128 devices in a mesh: row: 4 (over y), col: 16 (over x, z_lo, core), depth: 2 (over z_hi).
Axes of the slice: x: 4, y: 4, z: 4 (z_hi: 2, z_lo: 2; z = z_hi * 2 + z_lo), core: 2. Of those that a mesh axis runs over, the one named last changes fastest.
Arguments:
- sequence_stack: bfloat16 [256, 384, 64], P('depth', ('row', 'col')), may hold values from -6 to 6
- present_sequence_flags: int32 [256], replicated, may hold values 0 or 1
- genuine_residue_flags: int32 [384], replicated, may hold values 0 or 1
- couple_state: bfloat16 [384, 384, 128], P('row', 'col'), may hold values from -6 to 6
- tensor_scale: float32 [64], replicated, may hold values from 0.1 to 1.9
- tensor_entry_matrix: bfloat16 [64, 64], replicated, may hold values from -0.75 to 0.75
- tensor_final_matrix: bfloat16 [1024, 128], replicated, may hold values from -1 to 1
- tensor_offset: float32 [128], replicated, may hold values from -3 to 3
- mean_sequence_scale: float32 [64], replicated, may hold values from 0.1 to 1.9
- mean_couple_scale: float32 [128], replicated, may hold values from 0.1 to 1.9
- mean_score_matrix: float32 [128, 8], replicated, may hold values from -64 to 64
- mean_content_matrix: bfloat16 [64, 256], replicated, may hold values from -0.75 to 0.75
- mean_sigmoid_matrix: bfloat16 [64, 256], replicated, may hold values from -0.75 to 0.75
- mean_final_matrix: bfloat16 [256, 64], replicated, may hold values from -0.375 to 0.375
- trimul_scale: float32 [128], replicated, may hold values from 0.1 to 1.9
- trimul_entry_matrix: bfloat16 [128, 640], replicated, may hold values from -0.5 to 0.5
- trimul_result_scale: float32 [128], replicated, may hold values from 0.1 to 1.9
- trimul_final_matrix: bfloat16 [128, 128], replicated, may hold values from -0.5 to 0.5
Outputs:
- revised_sequences: bfloat16 [256, 384, 64], P('depth', ('row', 'col'))
- pair_output: bfloat16 [384, 384, 128], P('row', 'col')
The draws below stay inside these ranges and needn't reach their ends.
All inputs are finite; a program needn't handle non-finite values.
Results may differ from the reference program's by a relative error of at most 0.012.
The reference program's roundings to bfloat16 on the way count: a program that leaves them out, or rounds other values in their place, can miss the bound.
Values may be sent and summed in bfloat16 or wider, within the bound.
A program may use at most 128 MiB of HBM per device.

```python
import math
import jax
import jax.numpy as jnp
from jax import lax

SEQUENCE_WIDTH = 64
D_PAIR = 128
OPERAND_FEATURES = 32
MEAN_GROUPS = 8
GROUP_FEATURES = 32
COLUMN_TOKENS = 24
RESIDUE_COUNT = 384
SEQUENCE_COUNT = 256
N_COL = 16


def draw_mean_score_matrix(key, part):
    base = jnp.clip(jax.random.normal(key, (D_PAIR, MEAN_GROUPS), jnp.float32), -5.0, 5.0)
    spread = jnp.exp(jax.random.uniform(jax.random.fold_in(key, 7), (1, MEAN_GROUPS), jnp.float32, 0.0, 2.3))
    return base * spread * (1.0 / math.sqrt(D_PAIR))


def set_ends(result, rng, least, top_value):
    longest = result.shape.index(max(result.shape))
    spots = []
    for shift in (0, 1):
        where = [jax.random.randint(jax.random.fold_in(rng, axis), (), 0, length) for axis, length in enumerate(result.shape)]
        where[longest] = (where[longest] + shift) % result.shape[longest]
        spots.append(tuple(where))
    return result.at[spots[0]].set(least).at[spots[1]].set(top_value)


def level_of(rng, dims, shards, smallest, top_value):
    def one(position, parts):
        steps = jax.random.uniform(jax.random.fold_in(jax.random.fold_in(rng, 6), position), (parts,), jnp.float32, smallest / len(shards), top_value / len(shards))
        return jnp.repeat(jnp.exp(steps), dims[position] // parts).reshape((-1,) + (1,) * (len(dims) - position - 1))

    level = one(*shards[0])
    for cut in shards[1:]:
        level = level * one(*cut)
    return level


def scatter_about(key, dims, scale, reach, cuts=(), dtype=jnp.bfloat16):
    level = level_of(key, dims, cuts, -0.22, 0.18) if cuts else 1.0
    entries = jax.random.normal(key, dims, jnp.float32) * scale * level
    return jnp.minimum(jnp.maximum(entries, -reach), reach).astype(dtype)


def setup_inputs(seed: int = 0) -> dict:
    streams_of = jax.random.split(jax.random.key(seed), 19)
    sequence_stack = scatter_about(streams_of[0], (SEQUENCE_COUNT, RESIDUE_COUNT, SEQUENCE_WIDTH), 1.0, 6.0, ((0, 2), (1, 64)))
    present_sequence_flags = set_ends((jax.random.randint(streams_of[1], (SEQUENCE_COUNT,), 0, 4) < 3).astype(jnp.int32), jax.random.fold_in(streams_of[1], 1), 0, 1)
    genuine_residue_flags = set_ends((jax.random.randint(streams_of[2], (RESIDUE_COUNT,), 0, 8) < 7).astype(jnp.int32), jax.random.fold_in(streams_of[2], 1), 0, 1)
    couple_state = scatter_about(streams_of[3], (RESIDUE_COUNT, RESIDUE_COUNT, D_PAIR), 1.0, 6.0, ((0, 4), (1, 16)))
    tensor_scale = jnp.clip(1.0 + 0.18 * jax.random.normal(streams_of[4], (SEQUENCE_WIDTH,), jnp.float32), 0.1, 1.9)
    tensor_entry_matrix = scatter_about(streams_of[5], (SEQUENCE_WIDTH, 2 * OPERAND_FEATURES), SEQUENCE_WIDTH ** -0.5, 0.75)
    tensor_final_matrix = scatter_about(streams_of[6], (OPERAND_FEATURES * OPERAND_FEATURES, D_PAIR), OPERAND_FEATURES ** -0.5, 1.0)
    tensor_offset = scatter_about(streams_of[7], (D_PAIR,), 0.5, 3.0, (), jnp.float32)
    mean_sequence_scale = jnp.clip(1.0 + 0.18 * jax.random.normal(streams_of[8], (SEQUENCE_WIDTH,), jnp.float32), 0.1, 1.9)
    mean_couple_scale = jnp.clip(1.0 + 0.18 * jax.random.normal(streams_of[9], (D_PAIR,), jnp.float32), 0.1, 1.9)
    mean_score_matrix = draw_mean_score_matrix(jax.random.fold_in(streams_of[18], 71), 0)
    mean_content_matrix = scatter_about(streams_of[11], (SEQUENCE_WIDTH, MEAN_GROUPS * GROUP_FEATURES), SEQUENCE_WIDTH ** -0.5, 0.75)
    mean_sigmoid_matrix = scatter_about(streams_of[12], (SEQUENCE_WIDTH, MEAN_GROUPS * GROUP_FEATURES), SEQUENCE_WIDTH ** -0.5, 0.75)
    mean_final_matrix = scatter_about(streams_of[13], (MEAN_GROUPS * GROUP_FEATURES, SEQUENCE_WIDTH), (MEAN_GROUPS * GROUP_FEATURES) ** -0.5, 0.375)
    trimul_scale = jnp.clip(1.0 + 0.18 * jax.random.normal(streams_of[14], (D_PAIR,), jnp.float32), 0.1, 1.9)
    trimul_entry_matrix = scatter_about(streams_of[15], (D_PAIR, 5 * D_PAIR), D_PAIR ** -0.5, 0.5)
    trimul_result_scale = jnp.clip(1.0 + 0.18 * jax.random.normal(streams_of[16], (D_PAIR,), jnp.float32), 0.1, 1.9)
    trimul_final_matrix = scatter_about(streams_of[17], (D_PAIR, D_PAIR), D_PAIR ** -0.5, 0.5)
    return {"sequence_stack": sequence_stack, "present_sequence_flags": present_sequence_flags, "genuine_residue_flags": genuine_residue_flags, "couple_state": couple_state, "tensor_scale": tensor_scale, "tensor_entry_matrix": tensor_entry_matrix, "tensor_final_matrix": tensor_final_matrix, "tensor_offset": tensor_offset, "mean_sequence_scale": mean_sequence_scale, "mean_couple_scale": mean_couple_scale, "mean_score_matrix": mean_score_matrix, "mean_content_matrix": mean_content_matrix, "mean_sigmoid_matrix": mean_sigmoid_matrix, "mean_final_matrix": mean_final_matrix, "trimul_scale": trimul_scale, "trimul_entry_matrix": trimul_entry_matrix, "trimul_result_scale": trimul_result_scale, "trimul_final_matrix": trimul_final_matrix}


epsilon = 1e-05

def standardize_features(value_rows, scale):
    value_rows = value_rows.astype(jnp.float32)
    average = lax.optimization_barrier(jnp.mean(value_rows, -1, keepdims=True))
    centred = value_rows - average
    variance = lax.optimization_barrier(jnp.mean(centred * centred, -1, keepdims=True))
    return centred * lax.rsqrt(variance + epsilon) * scale

def reference(sequence_stack, present_sequence_flags, genuine_residue_flags, couple_state, tensor_scale, tensor_entry_matrix, tensor_final_matrix, tensor_offset, mean_sequence_scale, mean_couple_scale, mean_score_matrix, mean_content_matrix, mean_sigmoid_matrix, mean_final_matrix, trimul_scale, trimul_entry_matrix, trimul_result_scale, trimul_final_matrix):
    row_softmax_weight = present_sequence_flags.astype(jnp.float32)
    row_count = jnp.sum(row_softmax_weight)
    tensor_standardized = standardize_features(sequence_stack, tensor_scale).astype(jnp.bfloat16)
    factors = (jnp.dot(tensor_standardized, tensor_entry_matrix, preferred_element_type=jnp.float32) * row_softmax_weight[:, None, None]).astype(jnp.bfloat16)
    left_projection = factors[..., :OPERAND_FEATURES].astype(jnp.float32)
    right_proj = factors[..., OPERAND_FEATURES:].astype(jnp.float32)
    left_factor_blocks = jnp.transpose(left_projection.reshape(SEQUENCE_COUNT, N_COL, COLUMN_TOKENS, OPERAND_FEATURES), (1, 0, 2, 3))
    out_float = tensor_final_matrix.astype(jnp.float32)

    def outer_block(piece):
        outer_sum = jnp.einsum('sic,sjd->ijcd', piece, right_proj).reshape(COLUMN_TOKENS, RESIDUE_COUNT, OPERAND_FEATURES * OPERAND_FEATURES)
        return jnp.dot(outer_sum, out_float, precision=lax.Precision.HIGHEST)
    projected_outer = lax.map(outer_block, left_factor_blocks).reshape(RESIDUE_COUNT, RESIDUE_COUNT, D_PAIR)
    update = projected_outer / (row_count + 0.001) + tensor_offset
    pair_one = (couple_state.astype(jnp.float32) + update).astype(jnp.bfloat16)
    token_weight = genuine_residue_flags.astype(jnp.float32)
    logits = jnp.einsum('ijc,ch->ijh', standardize_features(pair_one, mean_couple_scale), mean_score_matrix, precision=lax.Precision.HIGHEST)
    logits = logits + 1000000000.0 * (token_weight - 1.0)[None, :, None]
    peak = lax.optimization_barrier(jnp.max(logits, axis=1, keepdims=True))
    expo = jnp.exp(logits - peak)
    weights = (expo / lax.optimization_barrier(jnp.sum(expo, axis=1, keepdims=True))).astype(jnp.bfloat16)
    mean_standardized = standardize_features(sequence_stack, mean_sequence_scale).astype(jnp.bfloat16)
    value_rows = jnp.dot(mean_standardized, mean_content_matrix, preferred_element_type=jnp.float32).astype(jnp.bfloat16)
    value_rows = value_rows.reshape(SEQUENCE_COUNT, RESIDUE_COUNT, MEAN_GROUPS, GROUP_FEATURES)
    gate_values = jax.nn.sigmoid(jnp.dot(mean_standardized, mean_sigmoid_matrix, preferred_element_type=jnp.float32))
    averaged_values = jnp.einsum('ijh,sjhe->sihe', weights.astype(jnp.float32), value_rows.astype(jnp.float32))
    gated_output = gate_values * averaged_values.reshape(SEQUENCE_COUNT, RESIDUE_COUNT, MEAN_GROUPS * GROUP_FEATURES)
    sequence_delta = jnp.dot(gated_output, mean_final_matrix.astype(jnp.float32), precision=lax.Precision.HIGHEST)
    revised_sequences = (sequence_stack.astype(jnp.float32) + sequence_delta).astype(jnp.bfloat16)
    tri_normed = standardize_features(pair_one, trimul_scale).astype(jnp.bfloat16)
    projected = jnp.dot(tri_normed, trimul_entry_matrix, preferred_element_type=jnp.float32)
    pair_mask = (token_weight[:, None] * token_weight[None, :])[..., None]
    width = D_PAIR
    tri_left = (jax.nn.sigmoid(projected[..., 0:width]) * projected[..., width:2 * width] * pair_mask).astype(jnp.bfloat16)
    tri_right = (jax.nn.sigmoid(projected[..., 2 * width:3 * width]) * projected[..., 3 * width:4 * width] * pair_mask).astype(jnp.bfloat16)
    out_gate = jax.nn.sigmoid(projected[..., 4 * width:5 * width])
    product = jnp.einsum('ikc,jkc->ijc', tri_left.astype(jnp.float32), tri_right.astype(jnp.float32))
    final = out_gate * jnp.dot(standardize_features(product, trimul_result_scale).astype(jnp.bfloat16), trimul_final_matrix, preferred_element_type=jnp.float32)
    pair_output = (pair_one.astype(jnp.float32) + final).astype(jnp.bfloat16)
    return (revised_sequences, pair_output)
```

```python
import jax
import jax.numpy as jnp
from jax import lax
from jax.sharding import PartitionSpec as P

epsilon = 1e-05


def sent_to_all(array, axis):
    size = lax.axis_size(axis)
    return lax.all_to_all(
        jnp.broadcast_to(array[None], (size, *array.shape)), axis, 0, 0, tiled=True
    )


def laid_out(tiles, dim):
    shape = list(tiles.shape[1:])
    shape[dim] *= tiles.shape[0]
    return jnp.moveaxis(tiles, 0, dim).reshape(shape)


def gathered_copies(array, axis, dim):
    tiles = sent_to_all(array, axis)
    return laid_out(tiles, dim)


def broadcast(array, axis, root):
    return lax.dynamic_index_in_dim(lax.all_gather(array, axis), root, 0, keepdims=False)


def taken_together(array, axis):
    return sent_to_all(array, axis).sum(axis=0)


def taken_together_2(array, axis):
    everything = sent_to_all(array, axis)
    return jnp.max(everything, axis=0)


def split_up(array, dim, size):
    before, after = (array.shape[:dim], array.shape[dim + 1 :])
    return jnp.moveaxis(array.reshape(*before, size, -1, *after), dim, 0)


def sum_at_owner(array, axis, dim):
    size = lax.axis_size(axis)
    tiles = lax.all_to_all(split_up(array, dim, size), axis, 0, 0, tiled=True)
    return jnp.sum(tiles.astype(jnp.float32), axis=0)


def standardize_features(value_rows, scale):
    value_rows = value_rows.astype(jnp.float32)
    average = jnp.mean(value_rows, -1, keepdims=True)
    centred = value_rows - average
    variance = jnp.mean(centred * centred, -1, keepdims=True)
    return centred * lax.rsqrt(variance + epsilon) * scale


def on_device(
    sequence_stack,
    present_sequence_flags,
    genuine_residue_flags,
    couple_state,
    tensor_scale,
    tensor_entry_matrix,
    tensor_final_matrix,
    tensor_offset,
    mean_sequence_scale,
    mean_couple_scale,
    mean_score_matrix,
    mean_content_matrix,
    mean_sigmoid_matrix,
    mean_final_matrix,
    trimul_scale,
    trimul_entry_matrix,
    trimul_result_scale,
    trimul_final_matrix,
):
    n_row = lax.axis_size("row")
    n_col = lax.axis_size("col")
    row_index = lax.axis_index("row")
    col_index = lax.axis_index("col")
    depth_position = lax.axis_index("depth")
    piece_rows, piece_columns, width = couple_state.shape
    sequence_count, shard_residues, ignored_quantity = sequence_stack.shape
    hidden = tensor_entry_matrix.shape[1] // 2
    head_split = mean_score_matrix.shape[1]
    head_channels = mean_content_matrix.shape[1] // head_split
    token_weight = genuine_residue_flags.astype(jnp.float32)
    mask_as_float = present_sequence_flags.astype(jnp.float32)
    row_softmax_weight = lax.dynamic_slice_in_dim(
        mask_as_float, depth_position * sequence_count, sequence_count
    )
    row_count = jnp.sum(mask_as_float)
    entire_sequences = gathered_copies(sequence_stack, "col", 1)
    root_row = col_index * n_row // n_col
    offset = col_index * piece_columns - root_row * piece_rows
    column_piece = lax.dynamic_slice_in_dim(entire_sequences, offset, piece_columns, 1)
    whole_cols = broadcast(column_piece, "row", root_row)
    opm_rows = standardize_features(entire_sequences, tensor_scale).astype(jnp.bfloat16)
    opm_cols = standardize_features(whole_cols, tensor_scale).astype(jnp.bfloat16)
    left_projection = (
        jnp.dot(opm_rows, tensor_entry_matrix[:, :hidden], preferred_element_type=jnp.float32)
        * row_softmax_weight[:, None, None]
    ).astype(jnp.bfloat16)
    right_proj = (
        jnp.dot(opm_cols, tensor_entry_matrix[:, hidden:], preferred_element_type=jnp.float32)
        * row_softmax_weight[:, None, None]
    ).astype(jnp.bfloat16)
    outer_sum = jnp.einsum(
        "sic,sjd->ijcd", left_projection, right_proj, preferred_element_type=jnp.float32
    )
    outer_sum = outer_sum.reshape(piece_rows, piece_columns, hidden * hidden)
    out_float = tensor_final_matrix.astype(jnp.float32)
    partial_proj = jnp.dot(outer_sum, out_float, precision=lax.Precision.HIGHEST)
    projected_total = taken_together(partial_proj, "depth")
    update = projected_total / (row_count + 0.001) + tensor_offset
    pair_one = (couple_state.astype(jnp.float32) + update).astype(jnp.bfloat16)
    row_tokens = lax.dynamic_slice_in_dim(token_weight, row_index * piece_rows, piece_rows)
    col_tokens = lax.dynamic_slice_in_dim(token_weight, col_index * piece_columns, piece_columns)
    logits = jnp.einsum(
        "ijc,ch->ijh",
        standardize_features(pair_one, mean_couple_scale),
        mean_score_matrix,
        precision=lax.Precision.HIGHEST,
    )
    logits = logits + 1000000000.0 * (col_tokens - 1.0)[None, :, None]
    peak = taken_together_2(jnp.max(logits, axis=1), "col")
    expo = jnp.exp(logits - peak[:, None, :])
    total = taken_together(jnp.sum(expo, axis=1), "col")
    weights = (expo / total[:, None, :]).astype(jnp.bfloat16)
    col_normed = standardize_features(whole_cols, mean_sequence_scale).astype(jnp.bfloat16)
    value_rows = jnp.dot(
        col_normed, mean_content_matrix, preferred_element_type=jnp.float32
    ).astype(jnp.bfloat16)
    value_rows = value_rows.reshape(sequence_count, piece_columns, head_split, head_channels)
    averaged_values = jnp.einsum(
        "ijh,sjhe->sihe", weights, value_rows, preferred_element_type=jnp.float32
    )
    averaged_values = averaged_values.reshape(
        sequence_count, piece_rows, head_split * head_channels
    )
    output_weight = mean_final_matrix.astype(jnp.float32)
    row_normed = standardize_features(entire_sequences, mean_sequence_scale).astype(jnp.bfloat16)
    gate_values = jax.nn.sigmoid(
        jnp.dot(row_normed, mean_sigmoid_matrix, preferred_element_type=jnp.float32)
    )
    partial_update = jnp.dot(
        gate_values * averaged_values, output_weight, precision=lax.Precision.HIGHEST
    )
    sequence_delta = sum_at_owner(partial_update.astype(jnp.bfloat16), "col", 1)
    revised_sequences = (sequence_stack.astype(jnp.float32) + sequence_delta).astype(jnp.bfloat16)
    tri_normed = standardize_features(pair_one, trimul_scale).astype(jnp.bfloat16)
    projected = jnp.dot(tri_normed, trimul_entry_matrix, preferred_element_type=jnp.float32)
    pair_mask = (row_tokens[:, None] * col_tokens[None, :])[..., None]
    tri_left = (
        jax.nn.sigmoid(projected[..., 0:width]) * projected[..., width : 2 * width] * pair_mask
    ).astype(jnp.bfloat16)
    tri_right = (
        jax.nn.sigmoid(projected[..., 2 * width : 3 * width])
        * projected[..., 3 * width : 4 * width]
        * pair_mask
    ).astype(jnp.bfloat16)
    out_gate = jax.nn.sigmoid(projected[..., 4 * width : 5 * width])
    axes = ("row", "col", "depth")
    n_depth = lax.axis_size("depth")
    half = piece_columns // n_depth
    both = jnp.stack([tri_left, tri_right], axis=0)
    both = lax.dynamic_slice_in_dim(both, depth_position * half, half, 2)
    by_channel = jnp.transpose(both, (3, 2, 0, 1))
    arrived = lax.all_to_all(by_channel, axes, 0, 0, tiled=True)
    arrived = arrived.reshape(n_row, n_col * n_depth * half, 2, piece_rows)
    channel_product = jnp.einsum(
        "akm,bkn->ambn", arrived[:, :, 0], arrived[:, :, 1], preferred_element_type=jnp.float32
    ).astype(jnp.bfloat16)
    channel_product = channel_product.reshape(n_row, piece_rows, n_col, piece_columns)
    outgoing = jnp.transpose(channel_product, (0, 2, 1, 3))[:, :, None]
    outgoing = jnp.broadcast_to(outgoing, (n_row, n_col, n_depth, piece_rows, piece_columns))
    outgoing = outgoing.reshape(n_row * n_col * n_depth, piece_rows, piece_columns)
    returned = lax.all_to_all(outgoing, axes, 0, 0, tiled=True)
    product = jnp.transpose(returned, (1, 2, 0)).astype(jnp.float32)
    final = out_gate * jnp.dot(
        standardize_features(product, trimul_result_scale).astype(jnp.bfloat16),
        trimul_final_matrix,
        preferred_element_type=jnp.float32,
    )
    pair_output = (pair_one.astype(jnp.float32) + final).astype(jnp.bfloat16)
    return (revised_sequences, pair_output)


def solution(mesh):
    placed = (
        P("depth", ("row", "col"), None),
        P(),
        P(),
        P("row", "col", None),
        P(),
        P(),
        P(),
        P(),
        P(),
        P(),
        P(),
        P(),
        P(),
        P(),
        P(),
        P(),
        P(),
        P(),
    )
    return jax.shard_map(
        on_device,
        mesh=mesh,
        in_specs=placed,
        out_specs=(P("depth", ("row", "col"), None), P("row", "col", None)),
        check_vma=False,
    )
```

```python
import functools

import jax
import jax.numpy as jnp
from jax import lax
from jax.experimental import pallas as pl
from jax.experimental.pallas import tpu as pltpu
from jax.sharding import PartitionSpec as P

MESH = pl.DeviceIdType.MESH
EPS = 1e-05
F32 = jnp.float32
BF16 = jnp.bfloat16
NR, NC, ND = 4, 16, 2
ALL = NR * NC * ND
TOK, PAD = 6, 8
COLS = 24


def nt(a, b):
    return lax.dot_general(a, b, (((1,), (1,)), ((), ())), preferred_element_type=F32)


def nn(a, b):
    return lax.dot_general(a, b, (((1,), (0,)), ((), ())), preferred_element_type=F32)


def tn(a, b):
    return lax.dot_general(a, b, (((0,), (0,)), ((), ())), preferred_element_type=F32)


def sigmoid(x):
    return 1.0 / (1.0 + jnp.exp(-x))


def split2(x):
    hi = x.astype(BF16)
    return hi, (x - hi.astype(F32)).astype(BF16)


def normed_rows(x):
    centred = x - jnp.mean(x, axis=0, keepdims=True)
    variance = jnp.mean(centred * centred, axis=0, keepdims=True)
    return centred * lax.rsqrt(variance + EPS)


def iota(rows, columns, dim):
    return lax.broadcasted_iota(jnp.int32, (rows, columns), dim)


def column_of(row, n):
    return jnp.broadcast_to(row, (n, row.shape[1])).T


def landed(ref, sem):
    pltpu.make_async_copy(ref, ref, sem).wait()


def kernel(
    x_tok, x_blk, couple, present, genuine, opm_gain, entry, final, offset_row, score_gain, score,
    tri_gain_row, tri, res_gain_row, res, seq_gain_row, content, gate_w, out_w,
    revised, pair_out,
    l_f32, l_msg, r_msg, l_buf, r_buf, outer, pair, gate4, tri_f32, tri_msg, tri_buf,
    logit, p_msg, st_msg, p_buf, st_buf, x_buf, xn_buf, v_buf, d_msg, d_buf,
    tl_all, tr_all, z_msg, z_buf, z_f32,
    ri_mask, cj_flag, final_t, offset, score_t, tri_gain, tri_t, res_gain, res_t,
    val_bd, gate_bd, out_bd,
    send, recv, plane_sem,
):
    r = lax.axis_index("row")
    c = lax.axis_index("col")
    d = lax.axis_index("depth")
    me = r * (NC * ND) + c * ND + d
    own = lax.rem(c, 8)
    half = c // 8
    core = lax.rem(c, 2)
    sibling = (r, c + 1 - 2 * core, d)

    def remote(src, dst, k, dev):
        pltpu.make_async_remote_copy(
            src, dst, send.at[k], recv.at[k], device_id=dev, device_id_type=MESH
        ).start()

    def local(src, dst, k):
        pltpu.make_async_copy(src, dst, recv.at[k]).start()

    def finish(k):
        if k >= 2:
            landed(l_buf.at[pl.ds(0, 7)], send.at[0])
            landed(l_buf.at[pl.ds(0, 8)], send.at[9])
            for _ in range(NR * ND - 1):
                landed(r_msg, send.at[1])
            landed(x_buf.at[0, pl.ds(0, 31)], send.at[2])
        if k >= 5:
            landed(tri_msg.at[pl.ds(0, ALL - 1)], send.at[3])
            landed(p_buf.at[pl.ds(0, NC - 1)], send.at[4])
            landed(st_buf.at[pl.ds(0, NC - 1)], send.at[5])
            landed(x_buf.at[0], send.at[10])

            @pl.when(core != d)
            def _():
                landed(p_msg, send.at[4])
                landed(st_msg, send.at[5])
        if k >= 8:
            landed(d_buf.at[pl.ds(0, 7)], send.at[6])
            landed(z_buf.at[pl.ds(0, ALL - 1)], send.at[7])

            @pl.when(half != core)
            def _():
                landed(d_msg.at[0], send.at[6])
        if k >= 2:
            @pl.when(half != d)
            def _():
                landed(l_msg, send.at[0])

            @pl.when((r * 4 + c // 4) != c)
            def _():
                landed(r_msg, send.at[1])
        if k >= 9:
            landed(pair_out.at[d], send.at[8])
            landed(pair_out.at[1 - d], recv.at[8])

    def prepare():
        flags = genuine[...].astype(F32)
        lane = iota(128, 128, 1)
        token = r * 96 + d * 48 + (lane // 16) * TOK + lax.rem(lane, PAD)
        valid = lax.rem(lane, PAD) < TOK
        ri = jnp.zeros((8, 128), F32)
        cj = jnp.zeros((COLS, 128), F32)
        for k in range(3):
            row = flags[k : k + 1].astype(BF16)
            pick = jnp.logical_and(iota(128, 128, 0) + k * 128 == token, valid)
            ri += nn(jnp.broadcast_to(row, (8, 128)), pick.astype(BF16))
            mine = iota(COLS, 128, 1) + k * 128 == c * COLS + iota(COLS, 128, 0)
            cj += nt(mine.astype(BF16), jnp.broadcast_to(row, (128, 128)))
        ri_mask[...] = ri
        cj_flag[...] = cj
        for k in range(2):
            part = final[:, k].reshape(512, 128).astype(F32)
            final_t[k * 128 : (k + 1) * 128, :] = part.T.astype(BF16)
        offset[...] = column_of(offset_row[...], 128)
        tri_gain[...] = column_of(tri_gain_row[...], 128)
        res_gain[...] = column_of(res_gain_row[...], 128)
        score_t[...] = score[...].T * score_gain[...]
        tri_t[...] = tri[...].astype(F32).T.astype(BF16)
        res_t[...] = res[...].astype(F32).T.astype(BF16)
        row, col = iota(256, 256, 0), iota(256, 256, 1)
        same = row // 64 == lax.rem(col // 32, 4)
        same_t = lax.rem(row // 32, 4) == col // 64
        spread = (iota(64, 256, 0) == lax.rem(iota(64, 256, 1), 64)).astype(BF16)
        out4 = nn(out_w[...], spread).astype(BF16)
        for hp in range(4):
            pick = (row == (2 * hp + col // 128) * 32 + lax.rem(col, 32)).astype(BF16)
            for w, out in ((content, val_bd), (gate_w, gate_bd)):
                rows4 = jnp.concatenate([nn(w[...], pick)] * 4, axis=0)
                out[hp] = jnp.where(same, rows4, 0.0).astype(BF16)
            pick_t = (col == (2 * hp + row // 128) * 32 + lax.rem(row, 32)).astype(BF16)
            out_bd[hp] = jnp.where(same_t, nn(pick_t, out4), 0.0).astype(BF16)

    barrier = pltpu.get_barrier_semaphore()

    def greet(k, _):
        p = lax.rem(c * ND + d + k, NC * ND)
        pl.semaphore_signal(barrier, inc=1, device_id=(r, p // 2, lax.rem(p, 2)), device_id_type=MESH)
        return 0

    lax.fori_loop(1, NC * ND, greet, 0)
    for k in range(1, NR):
        pl.semaphore_signal(barrier, inc=1, device_id=(lax.rem(r + k, NR), c, d), device_id_type=MESH)

    l_f32[...] = jnp.zeros_like(l_f32)
    here = present[...].astype(F32)
    s_mask = jnp.where(d == 0, here[0:1], here[1:2])
    inv_count = 1.0 / (jnp.sum(here, keepdims=True).reshape(1, 1) + 0.001)
    gain0 = column_of(opm_gain[...], 128)
    entry_t = entry[...].astype(F32).T.astype(BF16)
    for t in range(TOK):
        x = normed_rows(x_tok[t].astype(F32)) * gain0
        f = nn(entry_t, x.astype(BF16)) * s_mask
        l_f32[pl.ds(t, 32, stride=PAD), :] = f[:32]
        r_msg[t * 32 : (t + 1) * 32, :] = f[32:].astype(BF16)
    l_msg[...] = l_f32[...].reshape(16, 16, 128).astype(BF16)

    pl.semaphore_wait(barrier, NC * ND - 1 + NR - 1)
    for k in range(1, NR):
        pl.semaphore_signal(plane_sem, inc=1, device_id=(lax.rem(r + k, NR), c, d), device_id_type=MESH)

    lane_half = pl.ds(pl.multiple_of(d * 128, 128), 128)
    l_dst = l_buf.at[:, pl.ds(pl.multiple_of(own * 16, 16), 16), lane_half]
    self_l = half == d

    @pl.when(self_l)
    def _():
        local(l_msg, l_dst, 0)

    @pl.when(jnp.logical_not(self_l))
    def _():
        remote(l_msg, l_dst, 0, (r, c, half))

    def send_l(k, _):
        remote(l_msg, l_dst, 0, (r, lax.rem(c + 2 * k, NC), half))
        return 0

    lax.fori_loop(1, 8, send_l, 0)

    pl.semaphore_wait(plane_sem, NR - 1)

    c_t = r * 4 + c // 4
    r_dst = r_buf.at[pl.ds(pl.multiple_of(lax.rem(c, 4) * 192, 192), 192), lane_half]
    self_r = c_t == c

    @pl.when(self_r)
    def _():
        local(r_msg, r_dst, 1)

    @pl.when(jnp.logical_not(self_r))
    def _():
        remote(r_msg, r_dst, 1, (r, c_t, d))

    def send_r(k, _):
        remote(r_msg, r_dst, 1, (lax.rem(r + k // 2, NR), c_t, lax.rem(d + k, ND)))
        return 0

    lax.fori_loop(1, NR * ND, send_r, 0)

    prepare()

    landed(l_buf.at[pl.ds(0, 8)], recv.at[0])
    for k in range(4):
        block = l_buf.at[:, pl.ds(pl.multiple_of((2 * k + core) * 16, 16), 16), :]
        remote(block, block, 9, sibling)

    x_dst = x_buf.at[core, r * 8 + c // 2]
    local(x_blk.at[c // 2], x_dst, 2)

    def send_x(k, _):
        b = lax.rem(c // 2 + k // 4, 8)
        remote(x_blk.at[b], x_dst, 2, (lax.rem(r + k, NR), 2 * b + core, d))
        return 0

    lax.fori_loop(1, 32, send_x, 0)

    landed(r_buf, recv.at[1])
    landed(l_buf.at[pl.ds(0, 8)], recv.at[9])

    def outer_step(k, _):
        outer[k] = nt(r_buf[...], l_buf[k]).astype(BF16)
        return 0

    lax.fori_loop(0, 16, outer_step, 0)

    lane = lax.broadcasted_iota(jnp.int32, (128, 128), 1)
    first = lax.rem(lane // PAD, 2) == 0
    first4 = first[:4]
    is_left = lax.rem(lane // PAD, 2) == d
    logit[...] = jnp.full(logit.shape, -3e38, F32)
    score_hi, score_lo = split2(score_t[...])
    ri = ri_mask[0:1, :]
    score_both = jnp.concatenate([score_hi, score_lo], axis=0)

    def column(j, _):
        rhs = outer[:, pl.ds(pl.multiple_of(j * 32, 32), 32), :].reshape(512, 128)
        o = nn(final_t[...], rhs)
        t = jnp.where(first, o[:128], o[128:])
        u = t + jnp.where(first, pltpu.roll(t, 120, 1), pltpu.roll(t, 8, 1))
        one = (couple[j].astype(F32) + (u * inv_count + offset[...])).astype(BF16)
        pair[j] = one
        x = normed_rows(one.astype(F32))
        x_hi, x_lo = split2(x)
        two = nn(score_both, x_hi)
        flag = cj_flag[pl.ds(j, 1), :]
        lg = two[:8] + two[8:] + nn(score_hi, x_lo) + 1e9 * (flag - 1.0)
        m = j // TOK
        row = lax.rem(m, 2) * 16 + (m // 2) * PAD + lax.rem(j, TOK)
        logit[pl.ds(row, 4, stride=32), :] = jnp.where(first4, lg[:4], lg[4:])
        q = nn(tri_t[...], (x * tri_gain[...]).astype(BF16))
        sg = sigmoid(jnp.where(is_left, q[0:128], q[256:384]))
        tri = sg * jnp.where(is_left, q[128:256], q[384:512]) * (flag * ri)
        tri_f32[pl.ds(j, 128, stride=COLS), :] = tri
        gate4[j] = sigmoid(q[512:640])
        return 0

    lax.fori_loop(0, COLS, column, 0)

    tri_msg[...] = tri_f32[...].reshape(128, COLS, 128).astype(BF16)
    local(tri_msg.at[me], tri_buf.at[r, c, d], 3)

    def send_t(k, _):
        p = lax.rem(me + k, ALL)
        remote(tri_msg.at[p], tri_buf.at[r, c, d], 3, (p // 32, lax.rem(p // 2, NC), lax.rem(p, ND)))
        return 0

    lax.fori_loop(1, ALL, send_t, 0)

    lg = logit[...].reshape(4, 32, 128)
    top = jnp.max(lg, axis=1, keepdims=True)
    e = jnp.exp(lg - top)
    p_msg[...] = e.astype(BF16)
    st_msg[...] = jnp.concatenate([top[:, 0], jnp.sum(e, axis=1)], axis=0)
    self_p = core == d

    @pl.when(self_p)
    def _():
        local(p_msg, p_buf.at[c], 4)
        local(st_msg, st_buf.at[c], 5)

    @pl.when(jnp.logical_not(self_p))
    def _():
        dev = (r, c - core + d, d)
        remote(p_msg, p_buf.at[c], 4, dev)
        remote(st_msg, st_buf.at[c], 5, dev)

    def send_p(k, _):
        dev = (r, 2 * lax.rem(c // 2 + k // 2, 8) + d, lax.rem(d + k, ND))
        remote(p_msg, p_buf.at[c], 4, dev)
        remote(st_msg, st_buf.at[c], 5, dev)
        return 0

    lax.fori_loop(1, NC, send_p, 0)

    landed(x_buf.at[core], recv.at[2])
    remote(x_buf.at[core], x_buf.at[core], 10, sibling)

    landed(tri_buf, recv.at[3])
    first384 = lax.rem(lax.broadcasted_iota(jnp.int32, (384, 128), 1) // PAD, 2) == 0
    for k in range(NR):
        t0 = tri_buf[k, :, 0].astype(F32).reshape(384, 128)
        t1 = tri_buf[k, :, 1].astype(F32).reshape(384, 128)
        tl_all[:, k * 128 : (k + 1) * 128] = jnp.where(first384, t0, t1).astype(BF16)
        tr_all[:, k * 128 : (k + 1) * 128] = jnp.where(first384, t1, t0).astype(BF16)
    for k in range(NR):
        z = tn(tr_all[:, k * 128 : (k + 1) * 128], tl_all[...])
        for i in range(NR):
            zi = z[:, i * 128 : (i + 1) * 128]
            up, down = pltpu.roll(zi, 8, 1), pltpu.roll(zi, 120, 1)
            zi, up, down = (a.reshape(2, 2, 2, 2, PAD, 128) for a in (zi, up, down))
            mask = first[:8]
            keep = jnp.where(mask, zi[:, 0], up[:, 1])
            other = jnp.where(mask, down[:, 0], zi[:, 1])
            for hi in range(2):
                for lo in range(2):
                    to = k * 4 + hi * 2 + lo
                    z_msg[i, to, 0] = keep[lo, :, 1 - hi].reshape(16, 128).astype(BF16)
                    z_msg[i, to, 1] = other[lo, :, 1 - hi].reshape(16, 128).astype(BF16)
    local(z_msg.at[r, c, d], z_buf.at[me], 7)

    def send_z(k, _):
        p = lax.rem(me + k, ALL)
        dev = (p // 32, lax.rem(p // 2, NC), lax.rem(p, ND))
        remote(z_msg.at[dev[0], dev[1], dev[2]], z_buf.at[me], 7, dev)
        return 0

    lax.fori_loop(1, ALL, send_z, 0)

    landed(x_buf.at[1 - core], recv.at[10])
    landed(p_buf, recv.at[4])
    landed(st_buf, recv.at[5])
    ones_bd = (iota(256, 256, 0) // 64 == iota(256, 256, 1) // 64).astype(BF16)
    seq_gain = jnp.concatenate([seq_gain_row[...]] * 4, axis=1)
    for g in range(4):
        lanes = slice(g * 256, (g + 1) * 256)
        x = x_buf[:, :, :, lanes].astype(F32).reshape(512, 256)
        mean = nn(x.astype(BF16), ones_bd) * (1.0 / 64)
        centred = x - mean
        s_hi, s_lo = split2(centred * centred)
        variance = (nn(s_hi, ones_bd) + nn(s_lo, ones_bd)) * (1.0 / 64)
        xn = (centred * lax.rsqrt(variance + EPS) * seq_gain).astype(BF16)
        xn_buf[:, lanes] = xn
        for hp in range(4):
            v = nn(xn, val_bd[hp]).astype(BF16)
            v_buf[2 * hp, :, g * 128 : (g + 1) * 128] = v[:, :128]
            v_buf[2 * hp + 1, :, g * 128 : (g + 1) * 128] = v[:, 128:]

    tops = st_buf[:, 0:4, :]
    factor = jnp.exp(tops - jnp.max(tops, axis=0, keepdims=True))
    total = jnp.sum(factor * st_buf[:, 4:8, :], axis=0, keepdims=True)
    factor = factor / total
    averaged = [None] * 8
    for h in range(4):
        w = p_buf[:, h].astype(F32) * factor[:, h : h + 1, :]
        w = jnp.concatenate([w[:, :16].reshape(256, 128), w[:, 16:].reshape(256, 128)], axis=0).astype(BF16)
        for b in range(2):
            a = tn(w, v_buf[h + 4 * b]).reshape(4, 2, 2, PAD, 512)
            averaged[h + 4 * b] = jnp.concatenate([a[:, k, b].reshape(32, 512) for k in range(2)], axis=0)
    base = pl.multiple_of(r * 64 + core * 32, 32)
    for g in range(4):
        lanes = slice(g * 256, (g + 1) * 256)
        xi = jnp.concatenate([xn_buf[pl.ds(base + 256 * k, 32), lanes] for k in range(2)], axis=0)
        acc = jnp.zeros((64, 256), F32)
        for hp in range(4):
            gates = sigmoid(nn(xi, gate_bd[hp]))
            a = jnp.concatenate(
                [averaged[2 * hp + b][:, g * 128 : (g + 1) * 128] for b in range(2)], axis=1
            )
            hi, lo = split2(gates * a)
            acc += nn(hi, out_bd[hp]) + nn(lo, out_bd[hp])
        d_msg[:, :, lanes] = acc.reshape(8, PAD, 256).astype(BF16)

    self_d = half == core
    d_dst = d_buf.at[c // 2]
    d_first = d_msg.at[lax.rem(own, 2) * 4 + own // 2]

    @pl.when(self_d)
    def _():
        local(d_first, d_dst, 6)

    @pl.when(jnp.logical_not(self_d))
    def _():
        remote(d_first, d_dst, 6, (r, core * 8 + own, d))

    def send_d(k, _):
        o = lax.rem(own + k, 8)
        remote(d_msg.at[lax.rem(o, 2) * 4 + o // 2], d_dst, 6, (r, core * 8 + o, d))
        return 0

    lax.fori_loop(1, 8, send_d, 0)

    landed(z_buf, recv.at[7])
    z = z_buf[...].astype(F32)
    z_f32[...] = normed_rows(z).reshape(2048, 128)
    for m in range(2):
        for t in range(TOK):
            zq = z_f32[pl.ds(m * PAD + t, 128, stride=16), :] * res_gain[...]
            f = nn(res_t[...], zq.astype(BF16))
            j0, j1 = m * TOK + t, (2 + m) * TOK + t
            one = jnp.where(first, pair[j0].astype(F32), pair[j1].astype(F32))
            g4 = jnp.where(first, gate4[j0], gate4[j1])
            pair_out[d, m * TOK + t] = (one + g4 * f).T.astype(BF16)
    remote(pair_out.at[d], pair_out.at[d], 8, (r, c, 1 - d))

    landed(d_buf, recv.at[6])
    revised[...] = (x_blk[...].astype(F32) + d_buf[...].astype(F32)).astype(BF16)


    finish(9)


def on_device(
    sequence_stack, present_sequence_flags, genuine_residue_flags, couple_state,
    tensor_scale, tensor_entry_matrix, tensor_final_matrix, tensor_offset,
    mean_sequence_scale, mean_couple_scale, mean_score_matrix, mean_content_matrix,
    mean_sigmoid_matrix, mean_final_matrix, trimul_scale, trimul_entry_matrix,
    trimul_result_scale, trimul_final_matrix,
):
    d = lax.axis_index("depth")
    x_tok = jnp.transpose(sequence_stack, (1, 2, 0))
    x_blk = jnp.transpose(sequence_stack.reshape(8, 16, TOK, 64), (0, 2, 1, 3)).reshape(8, TOK, 1024)
    x_blk = jnp.pad(x_blk, ((0, 0), (0, PAD - TOK), (0, 0)))
    lane = jnp.arange(128)
    place = jnp.where(lane % PAD < TOK, (lane // 16) * TOK + lane % PAD, -1)
    spread = (jnp.arange(48)[:, None] == place[None, :]).astype(BF16)
    mine = lax.dynamic_slice_in_dim(couple_state, d * 48, 48, 0)
    couple = jnp.einsum("ijc,ip->jcp", mine, spread, preferred_element_type=F32).astype(BF16)
    vm = pl.BlockSpec(memory_space=pltpu.VMEM)
    row = lambda v: v.reshape(1, -1)
    args = (
        x_tok, x_blk, couple, present_sequence_flags.reshape(2, 128), genuine_residue_flags.reshape(3, 128),
        row(tensor_scale), tensor_entry_matrix, tensor_final_matrix.reshape(16, 2, 32, 128), row(tensor_offset),
        row(mean_couple_scale), mean_score_matrix, row(trimul_scale), trimul_entry_matrix,
        row(trimul_result_scale), trimul_final_matrix, row(mean_sequence_scale),
        mean_content_matrix, mean_sigmoid_matrix, mean_final_matrix,
    )
    V = pltpu.VMEM
    revised, pair_out = pl.pallas_call(
        kernel,
        name="msa_block",
        out_shape=(
            jax.ShapeDtypeStruct((8, PAD, 1024), BF16),
            jax.ShapeDtypeStruct((2, 12, 128, 128), BF16),
        ),
        in_specs=[vm] * len(args),
        out_specs=(vm, vm),
        scratch_shapes=[
            V((256, 128), F32), V((16, 16, 128), BF16), V((192, 128), BF16),
            V((16, 128, 256), BF16), V((768, 256), BF16), V((16, 768, 128), BF16),
            V((COLS, 128, 128), BF16), V((COLS, 128, 128), F32),
            V((128 * COLS, 128), F32), V((128, COLS, 128), BF16), V((NR, NC, ND, COLS, 128), BF16),
            V((128, 128), F32), V((4, 32, 128), BF16), V((8, 128), F32),
            V((NC, 4, 32, 128), BF16), V((NC, 8, 128), F32),
            V((2, 32, PAD, 1024), BF16), V((512, 1024), BF16), V((8, 512, 512), BF16),
            V((8, PAD, 1024), BF16), V((8, PAD, 1024), BF16),
            V((384, 512), BF16), V((384, 512), BF16),
            V((NR, NC, ND, 16, 128), BF16), V((128, 16, 128), BF16), V((2048, 128), F32),
            V((8, 128), F32), V((COLS, 128), F32), V((256, 512), BF16), V((128, 128), F32), V((8, 128), F32),
            V((128, 128), F32), V((640, 128), BF16), V((128, 128), F32), V((128, 128), BF16),
            V((4, 256, 256), BF16), V((4, 256, 256), BF16), V((4, 256, 256), BF16),
            pltpu.SemaphoreType.DMA((11,)), pltpu.SemaphoreType.DMA((11,)),
            pltpu.SemaphoreType.REGULAR,
        ],
        compiler_params=pltpu.CompilerParams(
            collective_id=0, has_side_effects=True, vmem_limit_bytes=56 * 1024 * 1024
        ),
    )(*args)
    revised = revised[:, :TOK].reshape(8, TOK, 16, 64)
    revised = jnp.transpose(revised, (0, 2, 1, 3)).reshape(128, TOK, 64)
    pair_out = pair_out.reshape(2, 2, TOK, 8, 2, PAD, 128)[:, :, :, :, :, :TOK]
    pair_out = jnp.transpose(pair_out, (0, 3, 5, 4, 1, 2, 6)).reshape(96, COLS, 128)
    return revised, pair_out


def solution(mesh):
    placed = (P("depth", ("row", "col"), None), P(), P(), P("row", "col", None)) + (P(),) * 14
    return jax.shard_map(
        on_device,
        mesh=mesh,
        in_specs=placed,
        out_specs=(P("depth", ("row", "col"), None), P("row", "col", None)),
        check_vma=False,
    )
```

```python
import functools

import jax
import jax.numpy as jnp
from jax import lax
from jax.experimental import pallas as pl
from jax.experimental.pallas import tpu as pltpu
from jax.sharding import PartitionSpec as P


MESH = pl.DeviceIdType.MESH
EPS = 1e-05
F32 = jnp.float32
BF16 = jnp.bfloat16
NR, NC, ND = 4, 16, 2
ALL = NR * NC * ND
TOK, PAD = 6, 8
COLS = 24
GROUP = 6


def nt(a, b):
    return lax.dot_general(a, b, (((1,), (1,)), ((), ())), preferred_element_type=F32)


def nn(a, b):
    return lax.dot_general(a, b, (((1,), (0,)), ((), ())), preferred_element_type=F32)


def tn(a, b):
    return lax.dot_general(a, b, (((0,), (0,)), ((), ())), preferred_element_type=F32)


def sigmoid(x):
    return 1.0 / (1.0 + jnp.exp(-x))


def split2(x):
    hi = x.astype(BF16)
    return hi, (x - hi.astype(F32)).astype(BF16)


def normed_rows(x):
    centred = x - jnp.mean(x, axis=0, keepdims=True)
    variance = jnp.mean(centred * centred, axis=0, keepdims=True)
    return centred * lax.rsqrt(variance + EPS)


def iota(rows, columns, dim):
    return lax.broadcasted_iota(jnp.int32, (rows, columns), dim)


def column_of(row, n):
    return jnp.broadcast_to(row, (n, row.shape[1])).T


def landed(ref, sem):
    pltpu.make_async_copy(ref, ref, sem).wait()


def kernel(
    x_tok, x_blk, couple, present, genuine, opm_gain, entry, final, offset_row, score_gain, score,
    tri_gain_row, tri, res_gain_row, res, seq_gain_row, content, gate_w, out_w,
    revised, pair_out,
    l_f32, l_msg, r_msg, l_buf, r_buf, outer, pair, gate4, tri_f32, tri_msg, tri_buf,
    logit, p_msg, st_msg, p_buf, st_buf, x_buf, xn_buf, v_buf, d_msg, d_buf,
    tl_all, tr_all, z_msg, z_buf, z_f32,
    ri_mask, cj_flag, final_t, offset, score_t, tri_gain, tri_t, res_gain, res_t,
    val_bd, gate_bd, out_bd, out_f32,
    send, recv, plane_sem,
):
    r = lax.axis_index("row")
    c = lax.axis_index("col")
    d = lax.axis_index("depth")
    me = r * (NC * ND) + c * ND + d
    own = lax.rem(c, 8)
    half = c // 8
    core = lax.rem(c, 2)
    sibling = (r, c + 1 - 2 * core, d)

    def remote(src, dst, k, dev):
        pltpu.make_async_remote_copy(
            src, dst, send.at[k], recv.at[k], device_id=dev, device_id_type=MESH
        ).start()

    def local(src, dst, k):
        pltpu.make_async_copy(src, dst, recv.at[k]).start()

    def finish(k):
        if k >= 2:
            landed(l_buf.at[pl.ds(0, 7)], send.at[0])
            landed(l_buf.at[pl.ds(0, 8)], send.at[9])
            landed(r_buf.at[pl.ds(0, 672)], send.at[11])
            landed(x_buf.at[0, pl.ds(0, 31)], send.at[2])
        if k >= 5:
            landed(tri_msg.at[pl.ds(0, ALL - 1)], send.at[3])
            landed(p_buf.at[pl.ds(0, NC - 1)], send.at[4])
            landed(st_buf.at[pl.ds(0, NC - 1)], send.at[5])
            landed(x_buf.at[0], send.at[10])

            @pl.when(core != d)
            def _():
                landed(p_msg, send.at[4])
                landed(st_msg, send.at[5])
        if k >= 8:
            landed(d_buf.at[pl.ds(0, 7)], send.at[6])
            landed(z_buf.at[pl.ds(0, ALL - 1)], send.at[7])

            @pl.when(half != core)
            def _():
                landed(d_msg.at[0], send.at[6])
        if k >= 2:
            @pl.when(half != d)
            def _():
                landed(l_msg, send.at[0])

            @pl.when(jnp.logical_not(jnp.logical_and(r * 4 + c // 4 == c, lax.rem(c, 4) == r)))
            def _():
                landed(r_msg, send.at[1])
        if k >= 9:
            landed(pair_out.at[pl.ds(0, 48)], send.at[8])
            landed(pair_out.at[pl.ds(0, 48)], recv.at[8])

    def prepare():
        flags = genuine[...].astype(F32)
        lane = iota(128, 128, 1)
        token = r * 96 + d * 48 + (lane // 16) * TOK + lax.rem(lane, PAD)
        valid = lax.rem(lane, PAD) < TOK
        ri = jnp.zeros((8, 128), F32)
        cj = jnp.zeros((COLS, 128), F32)
        for k in range(3):
            row = flags[k : k + 1].astype(BF16)
            pick = jnp.logical_and(iota(128, 128, 0) + k * 128 == token, valid)
            ri += nn(jnp.broadcast_to(row, (8, 128)), pick.astype(BF16))
            mine = iota(COLS, 128, 1) + k * 128 == c * COLS + iota(COLS, 128, 0)
            cj += nt(mine.astype(BF16), jnp.broadcast_to(row, (128, 128)))
        ri_mask[...] = ri
        cj_flag[...] = cj
        for k in range(2):
            part = final[:, k].reshape(512, 128).astype(F32)
            final_t[k * 128 : (k + 1) * 128, :] = part.T.astype(BF16)
        offset[...] = column_of(offset_row[...], 128)
        tri_gain[...] = column_of(tri_gain_row[...], 128)
        res_gain[...] = column_of(res_gain_row[...], 128)
        score_t[...] = score[...] * score_gain[...]
        tri_t[...] = tri[...].astype(F32).T.astype(BF16)
        res_t[...] = res[...].astype(F32).T.astype(BF16)
        row, col = iota(256, 256, 0), iota(256, 256, 1)
        same = row // 64 == lax.rem(col // 32, 4)
        same_t = lax.rem(row // 32, 4) == col // 64
        spread = (iota(64, 256, 0) == lax.rem(iota(64, 256, 1), 64)).astype(BF16)
        out4 = tn(out_w[...], spread).astype(BF16)
        for hp in range(4):
            pick = (row == (2 * hp + col // 128) * 32 + lax.rem(col, 32)).astype(BF16)
            for w, out in ((content, val_bd), (gate_w, gate_bd)):
                rows4 = jnp.concatenate([nn(w[...], pick)] * 4, axis=0)
                out[hp] = jnp.where(same, rows4, 0.0).astype(BF16)
            pick_t = (col == (2 * hp + row // 128) * 32 + lax.rem(row, 32)).astype(BF16)
            out_bd[hp] = jnp.where(same_t, nn(pick_t, out4), 0.0).astype(BF16)

    barrier = pltpu.get_barrier_semaphore()

    def greet(k, _):
        p = lax.rem(c * ND + d + k, NC * ND)
        pl.semaphore_signal(barrier, inc=1, device_id=(r, p // 2, lax.rem(p, 2)), device_id_type=MESH)
        return 0

    lax.fori_loop(1, NC * ND, greet, 0)
    for k in range(1, NR):
        pl.semaphore_signal(barrier, inc=1, device_id=(lax.rem(r + k, NR), c, d), device_id_type=MESH)

    l_f32[...] = jnp.zeros_like(l_f32)
    here = present[...].astype(F32)
    s_mask = jnp.where(d == 0, here[0:1], here[1:2])
    inv_count = 1.0 / (jnp.sum(here, keepdims=True).reshape(1, 1) + 0.001)
    gain0 = column_of(opm_gain[...], 128)
    entry_t = entry[...].astype(F32).T.astype(BF16)
    for t in range(TOK):
        x = normed_rows(x_tok[t].astype(F32)) * gain0
        f = nn(entry_t, x.astype(BF16)) * s_mask
        l_f32[pl.ds(t, 32, stride=PAD), :] = f[:32]
        r_msg[t * 32 : (t + 1) * 32, :] = f[32:].astype(BF16)
    l_msg[...] = l_f32[...].reshape(16, 16, 128).astype(BF16)

    pl.semaphore_wait(barrier, NC * ND - 1 + NR - 1)
    for k in range(1, NR):
        pl.semaphore_signal(plane_sem, inc=1, device_id=(lax.rem(r + k, NR), c, d), device_id_type=MESH)

    lane_half = pl.ds(pl.multiple_of(d * 128, 128), 128)
    l_dst = l_buf.at[:, pl.ds(pl.multiple_of(own * 16, 16), 16), lane_half]
    self_l = half == d

    @pl.when(self_l)
    def _():
        local(l_msg, l_dst, 0)

    @pl.when(jnp.logical_not(self_l))
    def _():
        remote(l_msg, l_dst, 0, (r, c, half))

    def send_l(k, _):
        remote(l_msg, l_dst, 0, (r, lax.rem(c + 2 * k, NC), half))
        return 0

    lax.fori_loop(1, 8, send_l, 0)

    pl.semaphore_wait(plane_sem, NR - 1)

    c_t = r * 4 + c // 4
    m_src = lax.rem(c, 4)
    r_dst = r_buf.at[pl.ds(pl.multiple_of(m_src * 192, 192), 192), lane_half]
    self_r = jnp.logical_and(c_t == c, m_src == r)

    @pl.when(self_r)
    def _():
        local(r_msg, r_dst, 1)

    @pl.when(jnp.logical_not(self_r))
    def _():
        remote(r_msg, r_dst, 1, (m_src, c_t, d))

    landed(r_msg, recv.at[1])
    r_mine = r_buf.at[pl.ds(pl.multiple_of(r * 192, 192), 192), lane_half]
    for k in range(1, NR * ND):
        remote(r_mine, r_mine, 11, (lax.rem(r + k // 2, NR), c, lax.rem(d + k, ND)))

    landed(l_buf.at[pl.ds(0, 8)], recv.at[0])
    for k in range(4):
        block = l_buf.at[:, pl.ds(pl.multiple_of((2 * k + core) * 16, 16), 16), :]
        remote(block, block, 9, sibling)

    x_dst = x_buf.at[core, r * 8 + c // 2]
    local(x_blk.at[c // 2], x_dst, 2)

    def send_x(k, _):
        b = lax.rem(c // 2 + k // 4, 8)
        remote(x_blk.at[b], x_dst, 2, (lax.rem(r + k, NR), 2 * b + core, d))
        return 0

    lax.fori_loop(1, 32, send_x, 0)

    prepare()

    landed(r_buf.at[pl.ds(0, 672)], recv.at[11])
    landed(l_buf.at[pl.ds(0, 8)], recv.at[9])

    def outer_step(k, _):
        o = nt(r_buf[...], l_buf[pl.ds(2 * k, 2)].reshape(256, 256)).astype(BF16)
        outer[2 * k] = o[:, :128]
        outer[2 * k + 1] = o[:, 128:]
        return 0

    lax.fori_loop(0, 8, outer_step, 0)

    lane = lax.broadcasted_iota(jnp.int32, (128, 128), 1)
    first = lax.rem(lane // PAD, 2) == 0
    first4 = first[:4]
    is_left = lax.rem(lane // PAD, 2) == d
    logit[...] = jnp.full(logit.shape, -3e38, F32)
    score_hi, score_lo = split2(score_t[...])
    ri = ri_mask[0:1, :]
    score_both = jnp.concatenate([score_hi, score_lo], axis=0)

    def columns(step, _):
        js = [step * GROUP + g for g in range(GROUP)]
        parts = [slice(g * 128, (g + 1) * 128) for g in range(GROUP)]
        wide = lambda blocks: jnp.concatenate(blocks, axis=1)
        rhs = wide([outer[:, pl.ds(pl.multiple_of(j * 32, 32), 32), :].reshape(512, 128) for j in js])
        o = nn(final_t[...], rhs)
        xs = []
        for j, part in zip(js, parts):
            t = jnp.where(first, o[:128, part], o[128:, part])
            u = t + jnp.where(first, pltpu.roll(t, 120, 1), pltpu.roll(t, 8, 1))
            one = (couple[j].astype(F32) + (u * inv_count + offset[...])).astype(BF16)
            pair[j] = one
            xs.append(normed_rows(one.astype(F32)))
        his, los = zip(*[split2(x) for x in xs])
        two = nn(score_both, wide(his))
        lgs = two[:8] + two[8:] + nn(score_hi, wide(los))
        qs = nn(tri_t[...], wide([(x * tri_gain[...]).astype(BF16) for x in xs]))
        for j, part in zip(js, parts):
            flag = cj_flag[pl.ds(j, 1), :]
            lg = lgs[:, part] + 1e9 * (flag - 1.0)
            m = j // TOK
            row = lax.rem(m, 2) * 16 + (m // 2) * PAD + lax.rem(j, TOK)
            logit[pl.ds(row, 4, stride=32), :] = jnp.where(first4, lg[:4], lg[4:])
            sg = sigmoid(jnp.where(is_left, qs[0:128, part], qs[256:384, part]))
            tri_f32[pl.ds(j, 128, stride=COLS), :] = (
                sg * jnp.where(is_left, qs[128:256, part], qs[384:512, part]) * (flag * ri)
            )
            gate4[j] = sigmoid(qs[512:640, part])
        return 0

    lax.fori_loop(0, COLS // GROUP, columns, 0)

    tri_msg[...] = tri_f32[...].reshape(128, COLS, 128).astype(BF16)
    local(tri_msg.at[me], tri_buf.at[r, c, d], 3)

    def send_t(k, _):
        p = lax.rem(me + k, ALL)
        remote(tri_msg.at[p], tri_buf.at[r, c, d], 3, (p // 32, lax.rem(p // 2, NC), lax.rem(p, ND)))
        return 0

    lax.fori_loop(1, ALL, send_t, 0)

    lg = logit[...].reshape(4, 32, 128)
    top = jnp.max(lg, axis=1, keepdims=True)
    e = jnp.exp(lg - top)
    p_msg[...] = e.astype(BF16)
    st_msg[...] = jnp.concatenate([top[:, 0], jnp.sum(e, axis=1)], axis=0)
    self_p = core == d

    @pl.when(self_p)
    def _():
        local(p_msg, p_buf.at[c], 4)
        local(st_msg, st_buf.at[c], 5)

    @pl.when(jnp.logical_not(self_p))
    def _():
        dev = (r, c - core + d, d)
        remote(p_msg, p_buf.at[c], 4, dev)
        remote(st_msg, st_buf.at[c], 5, dev)

    def send_p(k, _):
        dev = (r, 2 * lax.rem(c // 2 + k // 2, 8) + d, lax.rem(d + k, ND))
        remote(p_msg, p_buf.at[c], 4, dev)
        remote(st_msg, st_buf.at[c], 5, dev)
        return 0

    lax.fori_loop(1, NC, send_p, 0)

    landed(x_buf.at[core], recv.at[2])
    remote(x_buf.at[core], x_buf.at[core], 10, sibling)

    landed(tri_buf, recv.at[3])
    first384 = lax.rem(lax.broadcasted_iota(jnp.int32, (384, 128), 1) // PAD, 2) == 0
    for k in range(NR):
        t0 = tri_buf[k, :, 0].astype(F32).reshape(384, 128)
        t1 = tri_buf[k, :, 1].astype(F32).reshape(384, 128)
        tl_all[:, k * 128 : (k + 1) * 128] = jnp.where(first384, t0, t1).astype(BF16)
        tr_all[:, k * 128 : (k + 1) * 128] = jnp.where(first384, t1, t0).astype(BF16)
    for k in range(NR):
        z = tn(tr_all[:, k * 128 : (k + 1) * 128], tl_all[...])
        for i in range(NR):
            zi = z[:, i * 128 : (i + 1) * 128]
            up, down = pltpu.roll(zi, 8, 1), pltpu.roll(zi, 120, 1)
            zi, up, down = (a.reshape(2, 2, 2, 2, PAD, 128) for a in (zi, up, down))
            mask = first[:8]
            keep = jnp.where(mask, zi[:, 0], up[:, 1])
            other = jnp.where(mask, down[:, 0], zi[:, 1])
            for hi in range(2):
                for lo in range(2):
                    to = k * 4 + hi * 2 + lo
                    z_msg[i, to, 0] = keep[lo, :, 1 - hi].reshape(16, 128).astype(BF16)
                    z_msg[i, to, 1] = other[lo, :, 1 - hi].reshape(16, 128).astype(BF16)
    local(z_msg.at[r, c, d], z_buf.at[me], 7)

    def send_z(k, _):
        p = lax.rem(me + k, ALL)
        dev = (p // 32, lax.rem(p // 2, NC), lax.rem(p, ND))
        remote(z_msg.at[dev[0], dev[1], dev[2]], z_buf.at[me], 7, dev)
        return 0

    lax.fori_loop(1, ALL, send_z, 0)

    landed(x_buf.at[1 - core], recv.at[10])
    landed(p_buf, recv.at[4])
    landed(st_buf, recv.at[5])
    ones_bd = (iota(256, 256, 0) // 64 == iota(256, 256, 1) // 64).astype(BF16)
    seq_gain = jnp.concatenate([seq_gain_row[...]] * 4, axis=1)
    for g in range(4):
        lanes = slice(g * 256, (g + 1) * 256)
        x = x_buf[:, :, :, lanes].astype(F32).reshape(512, 256)
        mean = nn(x.astype(BF16), ones_bd) * (1.0 / 64)
        centred = x - mean
        s_hi, s_lo = split2(centred * centred)
        variance = (nn(s_hi, ones_bd) + nn(s_lo, ones_bd)) * (1.0 / 64)
        xn = (centred * lax.rsqrt(variance + EPS) * seq_gain).astype(BF16)
        xn_buf[:, lanes] = xn
        for hp in range(4):
            v = nn(xn, val_bd[hp]).astype(BF16)
            v_buf[2 * hp, :, g * 128 : (g + 1) * 128] = v[:, :128]
            v_buf[2 * hp + 1, :, g * 128 : (g + 1) * 128] = v[:, 128:]

    tops = st_buf[:, 0:4, :]
    factor = jnp.exp(tops - jnp.max(tops, axis=0, keepdims=True))
    total = jnp.sum(factor * st_buf[:, 4:8, :], axis=0, keepdims=True)
    factor = factor / total
    averaged = [None] * 8
    for h in range(4):
        w = p_buf[:, h].astype(F32) * factor[:, h : h + 1, :]
        w = jnp.concatenate([w[:, :16].reshape(256, 128), w[:, 16:].reshape(256, 128)], axis=0).astype(BF16)
        for b in range(2):
            a = tn(w, v_buf[h + 4 * b]).reshape(4, 2, 2, PAD, 512)
            averaged[h + 4 * b] = jnp.concatenate([a[:, k, b].reshape(32, 512) for k in range(2)], axis=0)
    base = pl.multiple_of(r * 64 + core * 32, 32)
    for g in range(4):
        lanes = slice(g * 256, (g + 1) * 256)
        xi = jnp.concatenate([xn_buf[pl.ds(base + 256 * k, 32), lanes] for k in range(2)], axis=0)
        acc = jnp.zeros((64, 256), F32)
        for hp in range(4):
            gates = sigmoid(nn(xi, gate_bd[hp]))
            a = jnp.concatenate(
                [averaged[2 * hp + b][:, g * 128 : (g + 1) * 128] for b in range(2)], axis=1
            )
            hi, lo = split2(gates * a)
            acc += nn(hi, out_bd[hp]) + nn(lo, out_bd[hp])
        d_msg[:, :, lanes] = acc.reshape(8, PAD, 256).astype(BF16)

    self_d = half == core
    d_dst = d_buf.at[c // 2]
    d_first = d_msg.at[lax.rem(own, 2) * 4 + own // 2]

    @pl.when(self_d)
    def _():
        local(d_first, d_dst, 6)

    @pl.when(jnp.logical_not(self_d))
    def _():
        remote(d_first, d_dst, 6, (r, core * 8 + own, d))

    def send_d(k, _):
        o = lax.rem(own + k, 8)
        remote(d_msg.at[lax.rem(o, 2) * 4 + o // 2], d_dst, 6, (r, core * 8 + o, d))
        return 0

    lax.fori_loop(1, 8, send_d, 0)

    landed(z_buf, recv.at[7])
    z = z_buf[...].astype(F32)
    z_f32[...] = normed_rows(z).reshape(2048, 128)
    row, lane = iota(96, 128, 0), iota(96, 128, 1)
    i, high = row % 48, row // 48
    compact = (lane == (i // TOK) * 16 + high * PAD + lax.rem(i, TOK)).astype(BF16)
    for m in range(2):
        for t in range(TOK):
            zq = z_f32[pl.ds(m * PAD + t, 128, stride=16), :] * res_gain[...]
            f = nn(res_t[...], zq.astype(BF16))
            j0, j1 = m * TOK + t, (2 + m) * TOK + t
            one = jnp.where(first, pair[j0].astype(F32), pair[j1].astype(F32))
            g4 = jnp.where(first, gate4[j0], gate4[j1])
            by_token = nt(compact, (one + g4 * f).astype(BF16))
            out_f32[pl.ds(j0, 48, stride=COLS), :] = by_token[:48]
            out_f32[pl.ds(j1, 48, stride=COLS), :] = by_token[48:]
    mine = pair_out.at[pl.ds(d * 48, 48)]
    mine[...] = out_f32[...].reshape(48, COLS, 128).astype(BF16)
    remote(mine, mine, 8, (r, c, 1 - d))

    landed(d_buf, recv.at[6])
    revised[...] = (x_blk[...].astype(F32) + d_buf[...].astype(F32)).astype(BF16)


    finish(9)


def on_device(
    sequence_stack, present_sequence_flags, genuine_residue_flags, couple_state,
    tensor_scale, tensor_entry_matrix, tensor_final_matrix, tensor_offset,
    mean_sequence_scale, mean_couple_scale, mean_score_matrix, mean_content_matrix,
    mean_sigmoid_matrix, mean_final_matrix, trimul_scale, trimul_entry_matrix,
    trimul_result_scale, trimul_final_matrix,
):
    d = lax.axis_index("depth")
    x_tok = jnp.transpose(sequence_stack, (1, 2, 0))
    x_blk = jnp.transpose(sequence_stack.reshape(8, 16, TOK, 64), (0, 2, 1, 3)).reshape(8, TOK, 1024)
    x_blk = jnp.pad(x_blk, ((0, 0), (0, PAD - TOK), (0, 0)))
    lane = jnp.arange(128)
    place = jnp.where(lane % PAD < TOK, (lane // 16) * TOK + lane % PAD, -1)
    spread = (jnp.arange(48)[:, None] == place[None, :]).astype(BF16)
    mine = lax.dynamic_slice_in_dim(couple_state, d * 48, 48, 0)
    couple = jnp.einsum("ijc,ip->jcp", mine, spread, preferred_element_type=F32).astype(BF16)
    vm = pl.BlockSpec(memory_space=pltpu.VMEM)
    row = lambda v: v.reshape(1, -1)
    args = (
        x_tok, x_blk, couple, present_sequence_flags.reshape(2, 128), genuine_residue_flags.reshape(3, 128),
        row(tensor_scale), tensor_entry_matrix, tensor_final_matrix.reshape(16, 2, 32, 128), row(tensor_offset),
        row(mean_couple_scale), mean_score_matrix.T, row(trimul_scale), trimul_entry_matrix,
        row(trimul_result_scale), trimul_final_matrix, row(mean_sequence_scale),
        mean_content_matrix, mean_sigmoid_matrix, mean_final_matrix.T,
    )
    V = pltpu.VMEM
    revised, pair_out = pl.pallas_call(
        kernel,
        name="msa_block",
        out_shape=(
            jax.ShapeDtypeStruct((8, PAD, 1024), BF16),
            jax.ShapeDtypeStruct((96, COLS, 128), BF16),
        ),
        in_specs=[vm] * len(args),
        out_specs=(vm, vm),
        scratch_shapes=[
            V((256, 128), F32), V((16, 16, 128), BF16), V((192, 128), BF16),
            V((16, 128, 256), BF16), V((768, 256), BF16), V((16, 768, 128), BF16),
            V((COLS, 128, 128), BF16), V((COLS, 128, 128), F32),
            V((128 * COLS, 128), F32), V((128, COLS, 128), BF16), V((NR, NC, ND, COLS, 128), BF16),
            V((128, 128), F32), V((4, 32, 128), BF16), V((8, 128), F32),
            V((NC, 4, 32, 128), BF16), V((NC, 8, 128), F32),
            V((2, 32, PAD, 1024), BF16), V((512, 1024), BF16), V((8, 512, 512), BF16),
            V((8, PAD, 1024), BF16), V((8, PAD, 1024), BF16),
            V((384, 512), BF16), V((384, 512), BF16),
            V((NR, NC, ND, 16, 128), BF16), V((128, 16, 128), BF16), V((2048, 128), F32),
            V((8, 128), F32), V((COLS, 128), F32), V((256, 512), BF16), V((128, 128), F32), V((8, 128), F32),
            V((128, 128), F32), V((640, 128), BF16), V((128, 128), F32), V((128, 128), BF16),
            V((4, 256, 256), BF16), V((4, 256, 256), BF16), V((4, 256, 256), BF16), V((48 * COLS, 128), F32),
            pltpu.SemaphoreType.DMA((12,)), pltpu.SemaphoreType.DMA((12,)),
            pltpu.SemaphoreType.REGULAR,
        ],
        compiler_params=pltpu.CompilerParams(
            collective_id=0, has_side_effects=True, vmem_limit_bytes=56 * 1024 * 1024
        ),
    )(*args)
    revised = revised[:, :TOK].reshape(8, TOK, 16, 64)
    revised = jnp.transpose(revised, (0, 2, 1, 3)).reshape(128, TOK, 64)
    return revised, pair_out


def solution(mesh):
    placed = (P("depth", ("row", "col"), None), P(), P(), P("row", "col", None)) + (P(),) * 14
    return jax.shard_map(
        on_device,
        mesh=mesh,
        in_specs=placed,
        out_specs=(P("depth", ("row", "col"), None), P("row", "col", None)),
        check_vma=False,
    )
```

```python
import functools

import jax
import jax.numpy as jnp
from jax import lax
from jax.experimental import pallas as pl
from jax.experimental.pallas import tpu as pltpu
from jax.sharding import PartitionSpec as P

MESH = pl.DeviceIdType.MESH
EPS = 1e-05
F32 = jnp.float32
BF16 = jnp.bfloat16
NR, NC, ND = 4, 16, 2
ALL = NR * NC * ND
TOK, PAD = 6, 8
COLS = 24
GROUP = 8


def nt(a, b):
    return lax.dot_general(a, b, (((1,), (1,)), ((), ())), preferred_element_type=F32)


def nn(a, b):
    return lax.dot_general(a, b, (((1,), (0,)), ((), ())), preferred_element_type=F32)


def tn(a, b):
    return lax.dot_general(a, b, (((0,), (0,)), ((), ())), preferred_element_type=F32)


def sigmoid(x):
    return 1.0 / (1.0 + jnp.exp(-x))


def split2(x):
    hi = x.astype(BF16)
    return hi, (x - hi.astype(F32)).astype(BF16)


def normed_rows(x):
    centred = x - jnp.mean(x, axis=0, keepdims=True)
    variance = jnp.mean(centred * centred, axis=0, keepdims=True)
    return centred * lax.rsqrt(variance + EPS)


def iota(rows, columns, dim):
    return lax.broadcasted_iota(jnp.int32, (rows, columns), dim)


def column_of(row, n):
    return jnp.broadcast_to(row, (n, row.shape[1])).T


def landed(ref, sem):
    pltpu.make_async_copy(ref, ref, sem).wait()


def kernel(
    x_tok, x_blk, couple, present, genuine, opm_gain, entry, final, offset_row, score_gain, score,
    tri_gain_row, tri, res_gain_row, res, seq_gain_row, content, gate_w, out_w,
    revised, pair_out,
    l_f32, l_msg, r_msg, l_buf, r_buf, outer, pair, gate4, tri_f32, tri_msg, tri_buf,
    logit, p_msg, st_msg, p_buf, st_buf, x_buf, xn_buf, v_buf, d_msg, d_buf,
    tl_all, tr_all, z_msg, z_buf, z_f32,
    ri_mask, cj_flag, final_t, offset, score_t, tri_gain, tri_t, res_gain, res_t,
    val_bd, gate_bd, out_bd, out_f32, couple_s, x_pad,
    send, recv, plane_sem,
):
    r = lax.axis_index("row")
    c = lax.axis_index("col")
    d = lax.axis_index("depth")
    me = r * (NC * ND) + c * ND + d
    own = lax.rem(c, 8)
    half = c // 8
    core = lax.rem(c, 2)
    sibling = (r, c + 1 - 2 * core, d)

    def remote(src, dst, k, dev):
        pltpu.make_async_remote_copy(
            src, dst, send.at[k], recv.at[k], device_id=dev, device_id_type=MESH
        ).start()

    def local(src, dst, k):
        pltpu.make_async_copy(src, dst, recv.at[k]).start()

    def finish(k):
        if k >= 2:
            landed(l_buf.at[pl.ds(0, 7)], send.at[0])
            landed(l_buf.at[pl.ds(0, 8)], send.at[9])
            landed(r_buf.at[pl.ds(0, 576)], send.at[11])
            landed(r_msg, send.at[1])
            landed(x_buf.at[0, pl.ds(0, 31)], send.at[2])
        if k >= 5:
            landed(tri_msg.at[pl.ds(0, ALL - 1)], send.at[3])
            landed(p_buf.at[pl.ds(0, NC - 1)], send.at[4])
            landed(st_buf.at[pl.ds(0, NC - 1)], send.at[5])
            landed(x_buf.at[0], send.at[10])

            @pl.when(core != d)
            def _():
                landed(p_msg, send.at[4])
                landed(st_msg, send.at[5])
        if k >= 8:
            landed(d_buf.at[pl.ds(0, 7)], send.at[6])
            landed(z_buf.at[pl.ds(0, ALL - 1)], send.at[7])

            @pl.when(half != core)
            def _():
                landed(d_msg.at[0], send.at[6])
        if k >= 2:
            @pl.when(half != d)
            def _():
                landed(l_msg, send.at[0])

            @pl.when(jnp.logical_not(jnp.logical_and(r * 4 + c // 4 == c, lax.rem(c, 4) == r)))
            def _():
                landed(r_msg, send.at[1])
        if k >= 9:
            landed(pair_out.at[pl.ds(0, 48)], send.at[8])
            landed(pair_out.at[pl.ds(0, 48)], recv.at[8])

    def send_x_all():
        x_dst = x_buf.at[core, r * 8 + c // 2]
        local(x_pad.at[c // 2], x_dst, 2)

        def send_x(k, _):
            b = lax.rem(c // 2 + k // 4, 8)
            remote(x_pad.at[b], x_dst, 2, (lax.rem(r + k, NR), 2 * b + core, d))
            return 0

        lax.fori_loop(1, 32, send_x, 0)

    def prepare_couple():
        out_f32[...] = couple[pl.ds(pl.multiple_of(d * 48, 48), 48)].astype(F32).reshape(48 * COLS, 128)
        lane = iota(48, 128, 1)
        valid = lax.rem(lane, PAD) < TOK
        spread = jnp.logical_and(iota(48, 128, 0) == (lane // 16) * TOK + lax.rem(lane, PAD), valid)
        spread = spread.astype(BF16)

        def some(step, _):
            for g in range(4):
                j = step * 4 + g
                tile = out_f32[pl.ds(j, 48, stride=COLS), :].astype(BF16)
                couple_s[j] = tn(tile, spread).astype(BF16)
            return 0

        lax.fori_loop(0, COLS // 4, some, 0)

    def prepare():
        flags = genuine[...].astype(F32)
        lane = iota(128, 128, 1)
        token = r * 96 + d * 48 + (lane // 16) * TOK + lax.rem(lane, PAD)
        valid = lax.rem(lane, PAD) < TOK
        ri = jnp.zeros((8, 128), F32)
        cj = jnp.zeros((COLS, 128), F32)
        for k in range(3):
            row = flags[k : k + 1].astype(BF16)
            pick = jnp.logical_and(iota(128, 128, 0) + k * 128 == token, valid)
            ri += nn(jnp.broadcast_to(row, (8, 128)), pick.astype(BF16))
            mine = iota(COLS, 128, 1) + k * 128 == c * COLS + iota(COLS, 128, 0)
            cj += nt(mine.astype(BF16), jnp.broadcast_to(row, (128, 128)))
        ri_mask[...] = ri
        cj_flag[...] = cj
        for k in range(2):
            part = final[:, k].reshape(512, 128).astype(F32)
            final_t[k * 128 : (k + 1) * 128, :] = part.T.astype(BF16)
        offset[...] = column_of(offset_row[...], 128)
        tri_gain[...] = column_of(tri_gain_row[...], 128)
        res_gain[...] = column_of(res_gain_row[...], 128)
        score_t[...] = score[...] * score_gain[...]
        tri_t[...] = tri[...].astype(F32).T.astype(BF16)
        res_t[...] = res[...].astype(F32).T.astype(BF16)
        row, col = iota(256, 256, 0), iota(256, 256, 1)
        same = row // 64 == lax.rem(col // 32, 4)
        same_t = lax.rem(row // 32, 4) == col // 64
        spread = (iota(64, 256, 0) == lax.rem(iota(64, 256, 1), 64)).astype(BF16)
        out4 = tn(out_w[...], spread).astype(BF16)
        for hp in range(4):
            pick = (row == (2 * hp + col // 128) * 32 + lax.rem(col, 32)).astype(BF16)
            for w, out in ((content, val_bd), (gate_w, gate_bd)):
                rows4 = jnp.concatenate([nn(w[...], pick)] * 4, axis=0)
                out[hp] = jnp.where(same, rows4, 0.0).astype(BF16)
            pick_t = (col == (2 * hp + row // 128) * 32 + lax.rem(row, 32)).astype(BF16)
            out_bd[hp] = jnp.where(same_t, nn(pick_t, out4), 0.0).astype(BF16)

    barrier = pltpu.get_barrier_semaphore()

    def greet(k, _):
        p = lax.rem(c * ND + d + k, NC * ND)
        pl.semaphore_signal(barrier, inc=1, device_id=(r, p // 2, lax.rem(p, 2)), device_id_type=MESH)
        return 0

    lax.fori_loop(1, NC * ND, greet, 0)
    for k in range(1, NR):
        pl.semaphore_signal(barrier, inc=1, device_id=(lax.rem(r + k, NR), c, d), device_id_type=MESH)

    l_f32[...] = jnp.zeros_like(l_f32)
    x_pad[...] = jnp.pad(x_blk[...], ((0, 0), (0, PAD - TOK), (0, 0)))
    here = present[...].astype(F32)
    s_mask = jnp.where(d == 0, here[0:1], here[1:2])
    inv_count = 1.0 / (jnp.sum(here, keepdims=True).reshape(1, 1) + 0.001)
    gain0 = column_of(opm_gain[...], 128)
    entry_t = entry[...].astype(F32).T.astype(BF16)
    for t in range(TOK):
        x = normed_rows(x_tok[t].astype(F32)) * gain0
        f = nn(entry_t, x.astype(BF16)) * s_mask
        l_f32[pl.ds(t, 32, stride=PAD), :] = f[:32]
        r_msg[t * 32 : (t + 1) * 32, :] = f[32:].astype(BF16)
    l_msg[...] = l_f32[...].reshape(16, 16, 128).astype(BF16)

    pl.semaphore_wait(barrier, NC * ND - 1 + NR - 1)
    for k in range(1, NR):
        pl.semaphore_signal(plane_sem, inc=1, device_id=(lax.rem(r + k, NR), c, d), device_id_type=MESH)

    lane_half = pl.ds(pl.multiple_of(d * 128, 128), 128)
    l_dst = l_buf.at[:, pl.ds(pl.multiple_of(own * 16, 16), 16), lane_half]
    self_l = half == d

    @pl.when(self_l)
    def _():
        local(l_msg, l_dst, 0)

    @pl.when(jnp.logical_not(self_l))
    def _():
        remote(l_msg, l_dst, 0, (r, c, half))

    def send_l(k, _):
        remote(l_msg, l_dst, 0, (r, lax.rem(c + 2 * k, NC), half))
        return 0

    lax.fori_loop(1, 8, send_l, 0)

    pl.semaphore_wait(plane_sem, NR - 1)

    c_t = r * 4 + c // 4
    m_src = lax.rem(c, 4)
    r_dst = r_buf.at[pl.ds(pl.multiple_of(m_src * 192, 192), 192), lane_half]
    self_r = jnp.logical_and(c_t == c, m_src == r)

    @pl.when(self_r)
    def _():
        local(r_msg, r_dst, 1)

    @pl.when(jnp.logical_not(self_r))
    def _():
        remote(r_msg, r_dst, 1, (m_src, c_t, d))

    remote(r_msg, r_dst, 1, (m_src, c_t, 1 - d))
    prepare_couple()
    r_mine = r_buf.at[pl.ds(pl.multiple_of(r * 192, 192), 192)]
    landed(r_mine, recv.at[1])
    for k in range(1, NR):
        remote(r_mine, r_mine, 11, (lax.rem(r + k, NR), c, d))

    landed(l_buf.at[pl.ds(0, 8)], recv.at[0])
    for k in range(4):
        block = l_buf.at[:, pl.ds(pl.multiple_of((2 * k + core) * 16, 16), 16), :]
        remote(block, block, 9, sibling)

    send_x_all()
    prepare()

    landed(r_buf.at[pl.ds(0, 576)], recv.at[11])
    landed(l_buf.at[pl.ds(0, 8)], recv.at[9])

    def outer_step(k, _):
        o = nt(r_buf[...], l_buf[pl.ds(2 * k, 2)].reshape(256, 256)).astype(BF16)
        outer[2 * k] = o[:, :128]
        outer[2 * k + 1] = o[:, 128:]
        return 0

    lax.fori_loop(0, 8, outer_step, 0)

    lane = lax.broadcasted_iota(jnp.int32, (128, 128), 1)
    first = lax.rem(lane // PAD, 2) == 0
    first4 = first[:4]
    is_left = lax.rem(lane // PAD, 2) == d
    logit[...] = jnp.full(logit.shape, -3e38, F32)
    score_hi, score_lo = split2(score_t[...])
    ri = ri_mask[0:1, :]
    score_both = jnp.concatenate([score_hi, score_lo], axis=0)

    def columns(step, _):
        js = [step * GROUP + g for g in range(GROUP)]
        parts = [slice(g * 128, (g + 1) * 128) for g in range(GROUP)]
        wide = lambda blocks: jnp.concatenate(blocks, axis=1)
        rhs = wide([outer[:, pl.ds(pl.multiple_of(j * 32, 32), 32), :].reshape(512, 128) for j in js])
        o = nn(final_t[...], rhs)
        xs = []
        for j, part in zip(js, parts):
            t = jnp.where(first, o[:128, part], o[128:, part])
            u = t + jnp.where(first, pltpu.roll(t, 120, 1), pltpu.roll(t, 8, 1))
            one = (couple_s[j].astype(F32) + (u * inv_count + offset[...])).astype(BF16)
            pair[j] = one
            xs.append(normed_rows(one.astype(F32)))
        his, los = zip(*[split2(x) for x in xs])
        two = nn(score_both, wide(his))
        lgs = two[:8] + two[8:] + nn(score_hi, wide(los))
        qs = nn(tri_t[...], wide([(x * tri_gain[...]).astype(BF16) for x in xs]))
        for j, part in zip(js, parts):
            flag = cj_flag[pl.ds(j, 1), :]
            lg = lgs[:, part] + 1e9 * (flag - 1.0)
            m = j // TOK
            row = lax.rem(m, 2) * 16 + (m // 2) * PAD + lax.rem(j, TOK)
            logit[pl.ds(row, 4, stride=32), :] = jnp.where(first4, lg[:4], lg[4:])
            sg = sigmoid(jnp.where(is_left, qs[0:128, part], qs[256:384, part]))
            tri_f32[pl.ds(j, 128, stride=COLS), :] = (
                sg * jnp.where(is_left, qs[128:256, part], qs[384:512, part]) * (flag * ri)
            )
            gate4[j] = sigmoid(qs[512:640, part])
        return 0

    lax.fori_loop(0, COLS // GROUP, columns, 0)

    tri_msg[...] = tri_f32[...].reshape(128, COLS, 128).astype(BF16)
    local(tri_msg.at[me], tri_buf.at[r, c, d], 3)

    def send_t(k, _):
        p = lax.rem(me + k, ALL)
        remote(tri_msg.at[p], tri_buf.at[r, c, d], 3, (p // 32, lax.rem(p // 2, NC), lax.rem(p, ND)))
        return 0

    lax.fori_loop(1, ALL, send_t, 0)

    lg = logit[...].reshape(4, 32, 128)
    top = jnp.max(lg, axis=1, keepdims=True)
    e = jnp.exp(lg - top)
    p_msg[...] = e.astype(BF16)
    st_msg[...] = jnp.concatenate([top[:, 0], jnp.sum(e, axis=1)], axis=0)
    self_p = core == d

    @pl.when(self_p)
    def _():
        local(p_msg, p_buf.at[c], 4)
        local(st_msg, st_buf.at[c], 5)

    @pl.when(jnp.logical_not(self_p))
    def _():
        dev = (r, c - core + d, d)
        remote(p_msg, p_buf.at[c], 4, dev)
        remote(st_msg, st_buf.at[c], 5, dev)

    def send_p(k, _):
        dev = (r, 2 * lax.rem(c // 2 + k // 2, 8) + d, lax.rem(d + k, ND))
        remote(p_msg, p_buf.at[c], 4, dev)
        remote(st_msg, st_buf.at[c], 5, dev)
        return 0

    lax.fori_loop(1, NC, send_p, 0)

    landed(x_buf.at[core], recv.at[2])
    remote(x_buf.at[core], x_buf.at[core], 10, sibling)

    landed(tri_buf, recv.at[3])
    first384 = lax.rem(lax.broadcasted_iota(jnp.int32, (384, 128), 1) // PAD, 2) == 0
    for k in range(NR):
        t0 = tri_buf[k, :, 0].astype(F32).reshape(384, 128)
        t1 = tri_buf[k, :, 1].astype(F32).reshape(384, 128)
        tl_all[:, k * 128 : (k + 1) * 128] = jnp.where(first384, t0, t1).astype(BF16)
        tr_all[:, k * 128 : (k + 1) * 128] = jnp.where(first384, t1, t0).astype(BF16)
    for k in range(NR):
        z = tn(tr_all[:, k * 128 : (k + 1) * 128], tl_all[...])
        for i in range(NR):
            zi = z[:, i * 128 : (i + 1) * 128]
            up, down = pltpu.roll(zi, 8, 1), pltpu.roll(zi, 120, 1)
            zi, up, down = (a.reshape(2, 2, 2, 2, PAD, 128) for a in (zi, up, down))
            mask = first[:8]
            keep = jnp.where(mask, zi[:, 0], up[:, 1])
            other = jnp.where(mask, down[:, 0], zi[:, 1])
            for hi in range(2):
                for lo in range(2):
                    to = k * 4 + hi * 2 + lo
                    z_msg[i, to, 0] = keep[lo, :, 1 - hi].reshape(16, 128).astype(BF16)
                    z_msg[i, to, 1] = other[lo, :, 1 - hi].reshape(16, 128).astype(BF16)
    local(z_msg.at[r, c, d], z_buf.at[me], 7)

    def send_z(k, _):
        p = lax.rem(me + k, ALL)
        dev = (p // 32, lax.rem(p // 2, NC), lax.rem(p, ND))
        remote(z_msg.at[dev[0], dev[1], dev[2]], z_buf.at[me], 7, dev)
        return 0

    lax.fori_loop(1, ALL, send_z, 0)

    landed(x_buf.at[1 - core], recv.at[10])
    landed(p_buf, recv.at[4])
    landed(st_buf, recv.at[5])
    ones_bd = (iota(256, 256, 0) // 64 == iota(256, 256, 1) // 64).astype(BF16)
    seq_gain = jnp.concatenate([seq_gain_row[...]] * 4, axis=1)
    for g in range(4):
        lanes = slice(g * 256, (g + 1) * 256)
        x = x_buf[:, :, :, lanes].astype(F32).reshape(512, 256)
        mean = nn(x.astype(BF16), ones_bd) * (1.0 / 64)
        centred = x - mean
        s_hi, s_lo = split2(centred * centred)
        variance = (nn(s_hi, ones_bd) + nn(s_lo, ones_bd)) * (1.0 / 64)
        xn = (centred * lax.rsqrt(variance + EPS) * seq_gain).astype(BF16)
        xn_buf[:, lanes] = xn
        for hp in range(4):
            v = nn(xn, val_bd[hp]).astype(BF16)
            v_buf[2 * hp, :, g * 128 : (g + 1) * 128] = v[:, :128]
            v_buf[2 * hp + 1, :, g * 128 : (g + 1) * 128] = v[:, 128:]

    tops = st_buf[:, 0:4, :]
    factor = jnp.exp(tops - jnp.max(tops, axis=0, keepdims=True))
    total = jnp.sum(factor * st_buf[:, 4:8, :], axis=0, keepdims=True)
    factor = factor / total
    averaged = [None] * 8
    for h in range(4):
        w = p_buf[:, h].astype(F32) * factor[:, h : h + 1, :]
        w = jnp.concatenate([w[:, :16].reshape(256, 128), w[:, 16:].reshape(256, 128)], axis=0).astype(BF16)
        for b in range(2):
            a = tn(w, v_buf[h + 4 * b]).reshape(4, 2, 2, PAD, 512)
            averaged[h + 4 * b] = jnp.concatenate([a[:, k, b].reshape(32, 512) for k in range(2)], axis=0)
    base = pl.multiple_of(r * 64 + core * 32, 32)
    for g in range(4):
        lanes = slice(g * 256, (g + 1) * 256)
        xi = jnp.concatenate([xn_buf[pl.ds(base + 256 * k, 32), lanes] for k in range(2)], axis=0)
        acc = jnp.zeros((64, 256), F32)
        for hp in range(4):
            gates = sigmoid(nn(xi, gate_bd[hp]))
            a = jnp.concatenate(
                [averaged[2 * hp + b][:, g * 128 : (g + 1) * 128] for b in range(2)], axis=1
            )
            hi, lo = split2(gates * a)
            acc += nn(hi, out_bd[hp]) + nn(lo, out_bd[hp])
        d_msg[:, :, lanes] = acc.reshape(8, PAD, 256).astype(BF16)

    self_d = half == core
    d_dst = d_buf.at[c // 2]
    d_first = d_msg.at[lax.rem(own, 2) * 4 + own // 2]

    @pl.when(self_d)
    def _():
        local(d_first, d_dst, 6)

    @pl.when(jnp.logical_not(self_d))
    def _():
        remote(d_first, d_dst, 6, (r, core * 8 + own, d))

    def send_d(k, _):
        o = lax.rem(own + k, 8)
        remote(d_msg.at[lax.rem(o, 2) * 4 + o // 2], d_dst, 6, (r, core * 8 + o, d))
        return 0

    lax.fori_loop(1, 8, send_d, 0)

    landed(z_buf, recv.at[7])
    z = z_buf[...].astype(F32)
    z_f32[...] = normed_rows(z).reshape(2048, 128)
    row, lane = iota(96, 128, 0), iota(96, 128, 1)
    i, high = row % 48, row // 48
    compact = (lane == (i // TOK) * 16 + high * PAD + lax.rem(i, TOK)).astype(BF16)
    for m in range(2):
        for t in range(TOK):
            zq = z_f32[pl.ds(m * PAD + t, 128, stride=16), :] * res_gain[...]
            f = nn(res_t[...], zq.astype(BF16))
            j0, j1 = m * TOK + t, (2 + m) * TOK + t
            one = jnp.where(first, pair[j0].astype(F32), pair[j1].astype(F32))
            g4 = jnp.where(first, gate4[j0], gate4[j1])
            by_token = nt(compact, (one + g4 * f).astype(BF16))
            out_f32[pl.ds(j0, 48, stride=COLS), :] = by_token[:48]
            out_f32[pl.ds(j1, 48, stride=COLS), :] = by_token[48:]
    mine = pair_out.at[pl.ds(d * 48, 48)]
    mine[...] = out_f32[...].reshape(48, COLS, 128).astype(BF16)
    remote(mine, mine, 8, (r, c, 1 - d))

    landed(d_buf, recv.at[6])
    revised[...] = (x_pad[...].astype(F32) + d_buf[...].astype(F32)).astype(BF16)[:, :TOK]


    finish(9)


def on_device(
    sequence_stack, present_sequence_flags, genuine_residue_flags, couple_state,
    tensor_scale, tensor_entry_matrix, tensor_final_matrix, tensor_offset,
    mean_sequence_scale, mean_couple_scale, mean_score_matrix, mean_content_matrix,
    mean_sigmoid_matrix, mean_final_matrix, trimul_scale, trimul_entry_matrix,
    trimul_result_scale, trimul_final_matrix,
):
    x_tok = jnp.transpose(sequence_stack, (1, 2, 0))
    x_blk = jnp.transpose(sequence_stack.reshape(8, 16, TOK, 64), (0, 2, 1, 3)).reshape(8, TOK, 1024)
    vm = pl.BlockSpec(memory_space=pltpu.VMEM)
    row = lambda v: v.reshape(1, -1)
    args = (
        x_tok, x_blk, couple_state, present_sequence_flags.reshape(2, 128), genuine_residue_flags.reshape(3, 128),
        row(tensor_scale), tensor_entry_matrix, tensor_final_matrix.reshape(16, 2, 32, 128), row(tensor_offset),
        row(mean_couple_scale), mean_score_matrix.T, row(trimul_scale), trimul_entry_matrix,
        row(trimul_result_scale), trimul_final_matrix, row(mean_sequence_scale),
        mean_content_matrix, mean_sigmoid_matrix, mean_final_matrix.T,
    )
    V = pltpu.VMEM
    revised, pair_out = pl.pallas_call(
        kernel,
        name="msa_block",
        out_shape=(
            jax.ShapeDtypeStruct((8, TOK, 1024), BF16),
            jax.ShapeDtypeStruct((96, COLS, 128), BF16),
        ),
        in_specs=[vm] * len(args),
        out_specs=(vm, vm),
        scratch_shapes=[
            V((256, 128), F32), V((16, 16, 128), BF16), V((192, 128), BF16),
            V((16, 128, 256), BF16), V((768, 256), BF16), V((16, 768, 128), BF16),
            V((COLS, 128, 128), BF16), V((COLS, 128, 128), F32),
            V((128 * COLS, 128), F32), V((128, COLS, 128), BF16), V((NR, NC, ND, COLS, 128), BF16),
            V((128, 128), F32), V((4, 32, 128), BF16), V((8, 128), F32),
            V((NC, 4, 32, 128), BF16), V((NC, 8, 128), F32),
            V((2, 32, PAD, 1024), BF16), V((512, 1024), BF16), V((8, 512, 512), BF16),
            V((8, PAD, 1024), BF16), V((8, PAD, 1024), BF16),
            V((384, 512), BF16), V((384, 512), BF16),
            V((NR, NC, ND, 16, 128), BF16), V((128, 16, 128), BF16), V((2048, 128), F32),
            V((8, 128), F32), V((COLS, 128), F32), V((256, 512), BF16), V((128, 128), F32), V((8, 128), F32),
            V((128, 128), F32), V((640, 128), BF16), V((128, 128), F32), V((128, 128), BF16),
            V((4, 256, 256), BF16), V((4, 256, 256), BF16), V((4, 256, 256), BF16), V((48 * COLS, 128), F32), V((COLS, 128, 128), BF16), V((8, PAD, 1024), BF16),
            pltpu.SemaphoreType.DMA((12,)), pltpu.SemaphoreType.DMA((12,)),
            pltpu.SemaphoreType.REGULAR,
        ],
        compiler_params=pltpu.CompilerParams(
            collective_id=0, has_side_effects=True, vmem_limit_bytes=56 * 1024 * 1024
        ),
    )(*args)
    revised = revised.reshape(8, TOK, 16, 64)
    revised = jnp.transpose(revised, (0, 2, 1, 3)).reshape(128, TOK, 64)
    return revised, pair_out


def solution(mesh):
    placed = (P("depth", ("row", "col"), None), P(), P(), P("row", "col", None)) + (P(),) * 14
    return jax.shard_map(
        on_device,
        mesh=mesh,
        in_specs=placed,
        out_specs=(P("depth", ("row", "col"), None), P("row", "col", None)),
        check_vma=False,
    )
```
